32 devices in a mesh: mp: 4 (over z), dp: 4 (over x, core), tensor: 2 (over y).
Axes of the slice: x: 2, y: 2, z: 4, core: 2. Of those that a mesh axis runs over, the one named last changes fastest.
Arguments:
- tokens: bfloat16 [1024, 8192], P(('mp', 'tensor'), 'dp'), may hold values from -64 to 64
- norm_gain: float32 [2, 8192], replicated, may hold values from 0.5 to 1.5
- gate_weight: bfloat16 [2, 8192, 14336], P(None, 'dp', ('mp', 'tensor')), may hold values from -0.0625 to 0.0625
- up_weight: bfloat16 [2, 8192, 14336], P(None, 'dp', ('mp', 'tensor')), may hold values from -0.0625 to 0.0625
- down_weight: bfloat16 [2, 14336, 8192], P(None, 'mp', 'tensor'), may hold values from -0.046875 to 0.046875
- sketch: bfloat16 [8192, 512], P('tensor'), may hold values from -6 to 6
Outputs:
- final_basis: float32 [8192, 512], P('tensor', ('mp', 'dp'))
- projected: float32 [8192, 512], P('tensor', ('mp', 'dp'))
The draws below stay inside these ranges and needn't reach their ends.
All inputs are finite; a program needn't handle non-finite values.
Results may differ from the reference program's by a relative error of at most 0.04.
Values may be sent and summed in bfloat16 or wider, within the bound.
No kernel may reach another device: no remote copies, remote signals or barrier semaphores. Data moves between devices by JAX's collectives and lax.ppermute only.
A program may use at most 192 MiB of HBM per device.

```python
import jax
import jax.numpy as jnp
from jax import lax

D = 8192
FFW = 14336
K = 512
TOKENS = 1024
N_DP = 4


def draw_tokens(key, part):
    first_key = jax.random.fold_in(key, 0)
    third_key = jax.random.fold_in(key, 2)
    normal_part = jnp.clip(jax.random.normal(first_key, (TOKENS, D), jnp.float32), -6.0, 6.0)
    position = jnp.arange(D, dtype=jnp.float32) / D
    jitter = jnp.exp(jax.random.uniform(third_key, (D,), jnp.float32, -0.5, 0.5))
    column_scale = jnp.exp(jnp.log(4.0) * (position - 0.5)) * jitter
    values = normal_part * column_scale[None, :]
    return values.astype(jnp.bfloat16)


def block_levels(key, dims, pieces, low, largest):
    level = 1.0
    for dim, shards_of in pieces:
        heights = jax.random.uniform(jax.random.fold_in(jax.random.fold_in(key, 6), dim), (shards_of,), jnp.float32, low / len(pieces), largest / len(pieces))
        level = level * jnp.repeat(jnp.exp(heights), dims[dim] // shards_of).reshape((-1,) + (1,) * (len(dims) - 1 - dim))
    return level


def gaussian(key, dims, spread, bound, pieces=(), kind=jnp.bfloat16):
    factor_of = block_levels(key, dims, pieces, -0.22, 0.18) if pieces else 1.0
    values = jax.random.normal(key, dims, jnp.float32) * spread * factor_of
    return jnp.minimum(jnp.maximum(values, -bound), bound).astype(kind)


def setup_inputs(seed: int = 0) -> dict:
    splits = jax.random.split(jax.random.key(seed), 7)
    tokens = draw_tokens(jax.random.fold_in(splits[6], 71), 0)
    norm_gain = jnp.clip(1.0 + 0.1 * jax.random.normal(splits[1], (2, D), jnp.float32), 0.5, 1.5)
    gate_weight = gaussian(splits[2], (2, D, FFW), D ** -0.5, 0.0625, ((1, 4), (2, 8)))
    up_weight = gaussian(splits[3], (2, D, FFW), D ** -0.5, 0.0625, ((1, 4), (2, 8)))
    down_weight = gaussian(splits[4], (2, FFW, D), FFW ** -0.5, 0.046875, ((1, 4), (2, 2)))
    sketch = gaussian(splits[5], (D, K), 1.0, 6.0, ((0, 2),))
    return dict(tokens=tokens, norm_gain=norm_gain, gate_weight=gate_weight, up_weight=up_weight, down_weight=down_weight, sketch=sketch)


EPSILON = 1e-05
HIGHEST = lax.Precision.HIGHEST

def orthonormal(matrix):
    gram_total = jnp.dot(matrix.T, matrix, precision=HIGHEST) / D
    lower_factor = jnp.linalg.cholesky(gram_total)
    return lax.linalg.triangular_solve(lower_factor, matrix, left_side=False, lower=True, transpose_a=True)

def sketch_product(left_acts, right_acts, matrix):
    inner_sums = jnp.dot(right_acts, matrix, precision=HIGHEST)
    return jnp.dot(left_acts.T, inner_sums, precision=HIGHEST) / TOKENS

def reference(tokens, norm_gain, gate_weight, up_weight, down_weight, sketch):
    values = tokens.astype(jnp.float32)
    inverse_root = lax.rsqrt(lax.optimization_barrier(jnp.sum(values * values, axis=1)) / D + EPSILON)
    normed = (values[None, :, :] * inverse_root[None, :, None] * norm_gain[:, None, :]).astype(jnp.bfloat16)
    block_width = D // N_DP

    def add_block(block_index, running):
        offset = (block_index * block_width).astype(jnp.int32)
        features_block = lax.dynamic_slice_in_dim(normed, offset, block_width, 2)
        gate_rows = lax.dynamic_slice_in_dim(gate_weight, offset, block_width, 1)
        up_rows = lax.dynamic_slice_in_dim(up_weight, offset, block_width, 1)
        outputs = []
        for copy_index in range(2):
            for weight_rows in (gate_rows, up_rows):
                product = jnp.dot(features_block[copy_index].astype(jnp.float32), weight_rows[copy_index].astype(jnp.float32), preferred_element_type=jnp.float32)
                rounded = lax.optimization_barrier(product.astype(jnp.bfloat16)).astype(jnp.float32)
                outputs.append(rounded)
        gate_sum = jnp.stack((outputs[0], outputs[2]))
        up_sum = jnp.stack((outputs[1], outputs[3]))
        return (running[0] + gate_sum, running[1] + up_sum)
    zeros_init = jnp.zeros((2, TOKENS, FFW), jnp.float32)
    gate_total, up_total = lax.fori_loop(0, N_DP, add_block, (zeros_init, zeros_init))
    hidden = (jax.nn.silu(gate_total) * up_total).astype(jnp.bfloat16)
    layer_out = [jnp.dot(hidden[copy_index].astype(jnp.float32), down_weight[copy_index].astype(jnp.float32), preferred_element_type=jnp.float32) for copy_index in range(2)]
    base_acts = layer_out[0]
    inst_acts = layer_out[1]
    first_basis = orthonormal(sketch_product(base_acts, inst_acts, sketch.astype(jnp.float32)))
    second_basis = orthonormal(sketch_product(inst_acts, base_acts, first_basis))
    final_basis = orthonormal(sketch_product(base_acts, inst_acts, second_basis))
    projected = sketch_product(inst_acts, base_acts, final_basis)
    return (final_basis, projected)
```

```python
import functools

import jax
import jax.numpy as jnp
from jax import lax
from jax.experimental import pallas as pl
from jax.experimental.pallas import tpu as pltpu
from jax.sharding import PartitionSpec as P

EPSILON = 1e-05
HIGH = lax.Precision.HIGH
HIGHEST = lax.Precision.HIGHEST
F32 = jnp.float32
BF16 = jnp.bfloat16
LEAF = 128


def swap(value, axis, bit):
    pairs = [(i, i ^ bit) for i in range(lax.axis_size(axis))]
    return lax.ppermute(value, axis, pairs)


def bits_of(axis):
    return [(axis, 1 << b) for b in range(lax.axis_size(axis).bit_length() - 1)]


def piece(value, index):
    return lax.dynamic_index_in_dim(value, index, 0, keepdims=False)


def leaf_inverse(block):
    size = block.shape[0]
    groups = [block[8 * g : 8 * g + 8, :] for g in range(size // 8)]
    lane = lax.broadcasted_iota(jnp.int32, (8, size), 1)
    sub = lax.broadcasted_iota(jnp.int32, (8, size), 0)
    pivots = []
    for j in range(size):
        home, row_at = divmod(j, 8)
        row = groups[home][row_at : row_at + 1, :]
        pivot = row[:, j : j + 1]
        inverse = 1.0 / pivot
        here = lane == j
        scaled = jnp.where(here, inverse, jnp.broadcast_to(row * inverse, (8, size)))
        for g in range(home, size // 8):
            old = groups[g]
            column = jnp.broadcast_to(old[:, j : j + 1], (8, size))
            new = jnp.where(here, 0.0, old) - column * scaled
            groups[g] = jnp.where(sub > row_at, new, old) if g == home else new
    out = []
    for g in range(size // 8):
        diagonal = jnp.sum(jnp.where(lane == sub + 8 * g, groups[g], 0.0), axis=1, keepdims=True)
        unit = jnp.where(lane == sub + 8 * g, 1.0, jnp.where(lane < sub + 8 * g, groups[g], 0.0))
        out.append(unit * lax.rsqrt(diagonal))
    return jnp.concatenate(out, axis=0)


def factor_kernel(gram_ref, out_ref, work_ref):
    size = gram_ref.shape[0]
    work_ref[...] = gram_ref[...]
    lane = lax.broadcasted_iota(jnp.int32, (LEAF, size), 1)

    def step(k, _):
        start = pl.multiple_of(k * LEAF, LEAF)
        rows = work_ref[pl.ds(start, LEAF), :]
        inverse = leaf_inverse(work_ref[pl.ds(start, LEAF), pl.ds(start, LEAF)])
        panel = jnp.dot(inverse, rows, precision=HIGHEST, preferred_element_type=F32)
        out_ref[pl.ds(start, LEAF), :] = jnp.where(lane < start, panel, 0.0)
        out_ref[pl.ds(start, LEAF), pl.ds(start, LEAF)] = inverse
        after = jnp.where(lane >= start + LEAF, panel, 0.0)
        work_ref[pl.ds(start, LEAF), :] = panel
        work_ref[pl.ds(start, LEAF), pl.ds(start, LEAF)] = inverse
        wide = work_ref[pl.ds(start, LEAF), :]
        work_ref[:, pl.ds(start, LEAF)] = jnp.zeros((size, LEAF), F32)
        work_ref[...] -= lax.dot_general(
            after, wide, (((0,), (0,)), ((), ())), precision=HIGHEST, preferred_element_type=F32
        )
        return 0

    lax.fori_loop(0, size // LEAF, step, 0)


def factor_inverse(gram):
    size = gram.shape[0]
    return pl.pallas_call(
        factor_kernel,
        out_shape=jax.ShapeDtypeStruct((size, size), F32),
        in_specs=[pl.BlockSpec(memory_space=pltpu.VMEM)],
        out_specs=pl.BlockSpec(memory_space=pltpu.VMEM),
        scratch_shapes=[pltpu.VMEM((size, size), F32)],
        cost_estimate=pl.CostEstimate(
            flops=100_000_000_000, bytes_accessed=8 * size * size, transcendentals=0
        ),
        name="factor_inverse",
    )(gram)


def down_kernel(hidden_ref, weight_ref, out_ref):
    out_ref[0] = jnp.dot(
        hidden_ref[...], weight_ref[0], preferred_element_type=F32
    ).astype(out_ref.dtype)


def down_project(hidden, down_weight, copy, pieces):
    rows, units = hidden.shape
    width = down_weight.shape[2] // pieces
    tile = min(width, 512)
    steps = width // tile
    return pl.pallas_call(
        down_kernel,
        grid=(pieces, steps),
        in_specs=[
            pl.BlockSpec((rows, units), lambda p, s: (0, 0)),
            pl.BlockSpec((1, units, tile), lambda p, s: (copy, 0, p * steps + s)),
        ],
        out_specs=pl.BlockSpec((1, rows, tile), lambda p, s: (p, 0, s)),
        out_shape=jax.ShapeDtypeStruct((pieces, rows, width), BF16),
        cost_estimate=pl.CostEstimate(
            flops=2 * rows * units * width * pieces,
            bytes_accessed=2 * units * width * pieces,
            transcendentals=0,
        ),
        name="down_project",
    )(hidden, down_weight)


def scatter_step(value, axis, bit):
    side = (lax.axis_index(axis) // bit) % 2
    halves = value.reshape((2, value.shape[0] // 2) + value.shape[1:])
    received = swap(piece(halves, 1 - side), axis, bit)
    return (piece(halves, side).astype(F32) + received.astype(F32)).astype(value.dtype)


def gather_step(value, axis, bit):
    side = (lax.axis_index(axis) // bit) % 2
    received = swap(value, axis, bit)
    first = jnp.where(side == 0, value, received)
    second = jnp.where(side == 0, received, value)
    return jnp.concatenate((first, second), axis=0)


def all_reduce(parts, orders):
    values = list(parts)
    for stage in range(len(orders[0])):
        values = [scatter_step(v, *o[stage]) for v, o in zip(values, orders, strict=True)]
    for stage in reversed(range(len(orders[0]))):
        values = [gather_step(v, *o[stage]) for v, o in zip(values, orders, strict=True)]
    return values


def split_dot(left, right):
    high = right.astype(BF16)
    low = (right - high.astype(F32)).astype(BF16)
    both = jnp.dot(left, jnp.concatenate((high, low), axis=1), preferred_element_type=F32)
    width = right.shape[1]
    return both[:, :width] + both[:, width:]


def on_device(tokens, norm_gain, gate_weight, up_weight, down_weight, sketch):
    dp, mp, tensor = lax.axis_size("dp"), lax.axis_size("mp"), lax.axis_size("tensor")
    me = lax.axis_index("dp")
    tokens_all = tokens.shape[0] * mp * tensor
    feature_count = tokens.shape[1]
    width = feature_count * dp
    group = tokens_all // dp

    local_gain = lax.dynamic_slice_in_dim(norm_gain, me * feature_count, feature_count, 1)
    local_values = tokens.astype(F32)
    local_total = lax.psum(jnp.sum(local_values * local_values, axis=1), "dp")
    local_root = lax.rsqrt(local_total / width + EPSILON)
    root_all = lax.all_gather(local_root, ("mp", "tensor"), axis=0, tiled=True)
    token_groups = lax.all_gather(tokens, ("mp", "tensor"), axis=0, tiled=True)
    token_groups = token_groups.reshape(dp, group, feature_count)
    root_groups = root_all.reshape(dp, group)

    def normed_rows(copy, offsets):
        rows = jnp.concatenate([piece(token_groups, me ^ j) for j in offsets], axis=0)
        roots = jnp.concatenate([piece(root_groups, me ^ j) for j in offsets], axis=0)
        return (rows.astype(F32) * roots[:, None] * local_gain[copy][None, :]).astype(BF16)

    def project(copy, offsets):
        rows = normed_rows(copy, offsets)
        gate = jnp.dot(rows, gate_weight[copy], preferred_element_type=F32).astype(BF16)
        up = jnp.dot(rows, up_weight[copy], preferred_element_type=F32).astype(BF16)
        return gate, up

    def hidden_of(copy):
        order = list(range(dp))
        held = None
        bit = 1
        while bit < dp:
            away = [j for j in order if j & bit]
            order = [j for j in order if not j & bit]
            if held is None:
                sent = project(copy, away)
                received = tuple(swap(v, "dp", bit) for v in sent)
                held = project(copy, order)
            else:
                split = held[0].shape[0] // 2
                received = tuple(swap(v[split:], "dp", bit) for v in held)
                held = tuple(v[:split] for v in held)
            held = tuple(a.astype(F32) + b.astype(F32) for a, b in zip(held, received, strict=True))
            bit *= 2
            if bit < dp:
                held = tuple(v.astype(BF16) for v in held)
        gate, up = held
        return (jax.nn.silu(gate) * up).astype(BF16)

    def gather_units(hidden):
        if tensor != 2:
            return lax.all_gather(hidden, "tensor", axis=1, tiled=True)
        other = swap(hidden, "tensor", 1)
        first = lax.axis_index("tensor") == 0
        return jnp.concatenate(
            (jnp.where(first, hidden, other), jnp.where(first, other, hidden)), axis=1
        )

    def acts_of(copy):
        hidden = gather_units(hidden_of(copy))
        partial = down_project(hidden, down_weight, copy, mp)
        summed = lax.psum_scatter(partial, "mp", scatter_dimension=0, tiled=False)
        blocks = summed.reshape(group, dp, -1).transpose(1, 0, 2)
        own = piece(blocks, me)
        arrived = [own] + [
            lax.ppermute(piece(blocks, me ^ j), "dp", [(i, i ^ j) for i in range(dp)])
            for j in range(1, dp)
        ]
        stacked = jnp.stack(arrived)
        bit = 1
        while bit < dp:
            turned = jnp.stack([stacked[j ^ bit] for j in range(dp)])
            stacked = jnp.where((me // bit) % 2 == 1, turned, stacked)
            bit *= 2
        return stacked.reshape(tokens_all, -1)

    inst = acts_of(1)
    base = acts_of(0)
    share = inst.shape[1]
    spot = lax.axis_index(("mp", "dp"))
    sketch_rows = lax.dynamic_slice_in_dim(sketch, spot * share, share, 0)
    rank = sketch.shape[1]

    def outer(value):
        return lax.dot_general(
            value, value, (((1,), (1,)), ((), ())), preferred_element_type=F32
        ).astype(BF16)

    first_inner = jnp.dot(inst, sketch_rows, preferred_element_type=F32).astype(BF16)
    base_outer = outer(base)
    core = bits_of("dp")[:1]
    far = bits_of("dp")[1:]
    ways = [
        core + far + bits_of("tensor") + bits_of("mp"),
        core + bits_of("tensor") + bits_of("mp") + far,
        core + bits_of("mp") + far + bits_of("tensor"),
    ]
    half = tokens_all // 2
    inner, outer_a, outer_b = all_reduce(
        (first_inner, base_outer[:, :half], base_outer[:, half:]), ways
    )
    base_outer = jnp.concatenate((outer_a, outer_b), axis=1)
    inst_outer = lax.psum(outer(inst), ("mp", "dp", "tensor"))

    scale = 1.0 / (tokens_all * tokens_all * width)

    def round_of(outer_matrix, inner_sums):
        moved = split_dot(outer_matrix, inner_sums)
        gram = lax.dot_general(
            inner_sums, moved, (((0,), (0,)), ((), ())), precision=HIGH
        ) * scale
        return moved, factor_inverse(gram)

    def turn(matrix, inverse):
        return lax.dot_general(matrix, inverse, (((1,), (1,)), ((), ())), precision=HIGH) / tokens_all

    moved, inverse = round_of(base_outer, inner.astype(F32))
    second_inner = turn(moved, inverse)
    moved, inverse = round_of(inst_outer, second_inner)
    third_inner = turn(moved, inverse)
    moved, inverse = round_of(base_outer, third_inner)
    basis_inner = turn(third_inner, inverse).astype(BF16)
    last_inner = (turn(moved, inverse) / tokens_all).astype(BF16)

    def outputs(inner_sums, acts):
        return lax.dot_general(
            inner_sums, acts, (((0,), (0,)), ((), ())), preferred_element_type=F32
        ).astype(BF16)

    both = jnp.stack((outputs(basis_inner, base), outputs(last_inner, inst)))
    shares = mp * dp
    both = both.reshape(2, shares, rank // shares, share).transpose(1, 0, 2, 3)
    both = lax.all_to_all(both, ("mp", "dp"), 0, 0, tiled=True)
    both = both.transpose(1, 0, 3, 2).reshape(2, shares * share, rank // shares).astype(F32)
    return both[0], both[1]


def solution(mesh):
    return jax.shard_map(
        on_device,
        mesh=mesh,
        in_specs=(
            P(("mp", "tensor"), "dp"),
            P(),
            P(None, "dp", ("mp", "tensor")),
            P(None, "dp", ("mp", "tensor")),
            P(None, "mp", "tensor"),
            P("tensor", None),
        ),
        out_specs=(P("tensor", ("mp", "dp")), P("tensor", ("mp", "dp"))),
        check_vma=False,
    )
```

```python
import functools

import jax
import jax.numpy as jnp
from jax import lax
from jax.experimental import pallas as pl
from jax.experimental.pallas import tpu as pltpu
from jax.sharding import PartitionSpec as P

EPSILON = 1e-05
HIGH = lax.Precision.HIGH
HIGHEST = lax.Precision.HIGHEST
F32 = jnp.float32
BF16 = jnp.bfloat16
LEAF = 128
CHUNKS = 2


def swap(value, axis, bit):
    pairs = [(i, i ^ bit) for i in range(lax.axis_size(axis))]
    return lax.ppermute(value, axis, pairs)


def bits_of(axis):
    return [(axis, 1 << b) for b in range(lax.axis_size(axis).bit_length() - 1)]


def after(value, others):
    return lax.optimization_barrier((value, others))[0]


def piece(value, index):
    return lax.dynamic_index_in_dim(value, index, 0, keepdims=False)


def leaf_inverse(block):
    size = block.shape[0]
    count = size // 8
    shape = (8, size)
    groups = [block[8 * g : 8 * g + 8, :] for g in range(count)]
    lane = lax.broadcasted_iota(jnp.int32, shape, 1)
    sub = lax.broadcasted_iota(jnp.int32, shape, 0)
    done = []
    for q in range(count):
        base = 8 * q
        own = groups[q]
        inside = (lane >= base) & (lane < base + 8)
        rows = [jnp.broadcast_to(own[i : i + 1, :], shape) for i in range(8)]
        a = {
            (i, k): jnp.broadcast_to(rows[i][:, base + k : base + k + 1], shape)
            for i in range(8)
            for k in range(i + 1)
        }
        columns = {
            (g, k): jnp.broadcast_to(groups[g][:, base + k : base + k + 1], shape)
            for g in range(q + 1, count)
            for k in range(8)
        }
        inverse, lower = [], {}
        for k in range(8):
            inverse.append(1.0 / a[k, k])
            for i in range(k + 1, 8):
                lower[i, k] = a[i, k] * inverse[k]
            for i in range(k + 1, 8):
                for m in range(k + 1, i + 1):
                    a[i, m] = a[i, m] - lower[i, k] * a[m, k]
        solved = []
        for i in range(8):
            value = jnp.where(inside, jnp.where(lane == base + i, 1.0, 0.0), rows[i])
            for k in range(i):
                value = value - lower[i, k] * solved[k]
            solved.append(value)
        turned = [None] * 8
        for k in reversed(range(8)):
            value = solved[k] * inverse[k]
            for i in reversed(range(k + 1, 8)):
                value = value - lower[i, k] * turned[i]
            turned[k] = value
        for g in range(q + 1, count):
            value = jnp.where(inside, 0.0, groups[g])
            for k in range(8):
                value = value - columns[g, k] * turned[k]
            groups[g] = value
        joined = solved[0] * lax.rsqrt(a[0, 0])
        for i in range(1, 8):
            joined = jnp.where(sub == i, solved[i] * lax.rsqrt(a[i, i]), joined)
        done.append(jnp.where(lane <= sub + base, joined, 0.0))
    return jnp.concatenate(done, axis=0)


def factor_kernel(gram_ref, out_ref, work_ref):
    size = gram_ref.shape[0]
    count = size // LEAF
    work_ref[...] = gram_ref[...]
    lane = lax.broadcasted_iota(jnp.int32, (LEAF, size), 1)

    def step(k, _):
        start = pl.multiple_of(k * LEAF, LEAF)
        here = pl.ds(start, LEAF)
        inverse = leaf_inverse(work_ref[here, here])
        panel = jnp.dot(
            inverse, work_ref[here, :], precision=HIGHEST, preferred_element_type=F32
        )
        out_ref[here, :] = jnp.where(lane < start, panel, 0.0)
        out_ref[here, here] = inverse
        work_ref[here, :] = panel
        work_ref[here, here] = inverse
        for at in range(count - 1):

            @pl.when(k == at)
            def _(at=at):
                old, cut = at * LEAF, (at + 1) * LEAF
                change = lax.dot_general(
                    work_ref[old:cut, cut:],
                    work_ref[old:cut, :],
                    (((0,), (0,)), ((), ())),
                    precision=HIGHEST,
                    preferred_element_type=F32,
                )
                if at:
                    work_ref[cut:, :old] -= change[:, :old]
                work_ref[cut:, old:cut] = -change[:, old:cut]
                work_ref[cut:, cut:] -= change[:, cut:]

        return 0

    lax.fori_loop(0, count, step, 0)


def factor_inverse(gram):
    size = gram.shape[0]
    return pl.pallas_call(
        factor_kernel,
        out_shape=jax.ShapeDtypeStruct((size, size), F32),
        in_specs=[pl.BlockSpec(memory_space=pltpu.VMEM)],
        out_specs=pl.BlockSpec(memory_space=pltpu.VMEM),
        scratch_shapes=[pltpu.VMEM((size, size), F32)],
        cost_estimate=pl.CostEstimate(
            flops=20_000_000_000, bytes_accessed=8 * size * size, transcendentals=0
        ),
        name="factor_inverse",
    )(gram)


def down_kernel(hidden_ref, weight_ref, out_ref):
    out_ref[0] = jnp.dot(
        hidden_ref[...], weight_ref[0], preferred_element_type=F32
    ).astype(out_ref.dtype)


def down_project(hidden, down_weight, copy, pieces):
    rows, units = hidden.shape
    width = down_weight.shape[2] // pieces
    tile = min(width, 512)
    steps = width // tile
    return pl.pallas_call(
        down_kernel,
        grid=(pieces, steps),
        in_specs=[
            pl.BlockSpec((rows, units), lambda p, s: (0, 0)),
            pl.BlockSpec((1, units, tile), lambda p, s: (copy, 0, p * steps + s)),
        ],
        out_specs=pl.BlockSpec((1, rows, tile), lambda p, s: (p, 0, s)),
        out_shape=jax.ShapeDtypeStruct((pieces, rows, width), BF16),
        cost_estimate=pl.CostEstimate(
            flops=2 * rows * units * width * pieces,
            bytes_accessed=2 * units * width * pieces,
            transcendentals=0,
        ),
        name="down_project",
    )(hidden, down_weight)


def scatter_step(value, axis, bit):
    side = (lax.axis_index(axis) // bit) % 2
    halves = value.reshape((2, value.shape[0] // 2) + value.shape[1:])
    received = swap(piece(halves, 1 - side), axis, bit)
    return (piece(halves, side).astype(F32) + received.astype(F32)).astype(value.dtype)


def gather_step(value, axis, bit):
    side = (lax.axis_index(axis) // bit) % 2
    received = swap(value, axis, bit)
    first = jnp.where(side == 0, value, received)
    second = jnp.where(side == 0, received, value)
    return jnp.concatenate((first, second), axis=0)


def reduce_halves(value, order):
    steps = []
    for pair in order:
        value = scatter_step(value, *pair)
        steps.append(value)
    return value, steps


def gather_halves(value, order):
    for pair in reversed(order):
        value = gather_step(value, *pair)
    return value


def split_dot(left, right):
    high = right.astype(BF16)
    low = (right - high.astype(F32)).astype(BF16)
    both = jnp.dot(left, jnp.concatenate((high, low), axis=1), preferred_element_type=F32)
    width = right.shape[1]
    return both[:, :width] + both[:, width:]


def on_device(tokens, norm_gain, gate_weight, up_weight, down_weight, sketch):
    dp, mp, tensor = lax.axis_size("dp"), lax.axis_size("mp"), lax.axis_size("tensor")
    me = lax.axis_index("dp")
    tokens_all = tokens.shape[0] * mp * tensor
    feature_count = tokens.shape[1]
    width = feature_count * dp

    local_gain = lax.dynamic_slice_in_dim(norm_gain, me * feature_count, feature_count, 1)
    local_values = tokens.astype(F32)
    local_total = lax.psum(jnp.sum(local_values * local_values, axis=1), "dp")
    local_root = lax.rsqrt(local_total / width + EPSILON)
    root_all = lax.all_gather(local_root, ("mp", "tensor"), axis=0, tiled=True)
    rows_each = tokens.shape[0] // CHUNKS
    group = tokens_all // dp // CHUNKS
    token_groups = [
        lax.all_gather(
            tokens[h * rows_each : (h + 1) * rows_each], ("mp", "tensor"), axis=0, tiled=True
        ).reshape(dp, group, feature_count)
        for h in range(CHUNKS)
    ]
    roots = root_all.reshape(-1, CHUNKS, rows_each)
    root_groups = [roots[:, h].reshape(dp, group) for h in range(CHUNKS)]

    def project(copy, chunk, offsets, groups):
        rows = jnp.concatenate([piece(groups, me ^ j) for j in offsets], axis=0)
        roots = jnp.concatenate([piece(root_groups[chunk], me ^ j) for j in offsets], axis=0)
        rows = (rows.astype(F32) * roots[:, None] * local_gain[copy][None, :]).astype(BF16)
        gate = jnp.dot(rows, gate_weight[copy], preferred_element_type=F32).astype(BF16)
        up = jnp.dot(rows, up_weight[copy], preferred_element_type=F32).astype(BF16)
        return gate, up

    def near_sum(copy, chunk, groups):
        sent = project(copy, chunk, list(range(1, dp, 2)), groups)
        received = tuple(swap(v, "dp", 1) for v in sent)
        held = project(copy, chunk, list(range(0, dp, 2)), after(groups, sent))
        return tuple(
            (a.astype(F32) + b.astype(F32)).astype(BF16)
            for a, b in zip(held, received, strict=True)
        )

    def hidden_of(held):
        bit = 2
        while bit < dp:
            split = held[0].shape[0] // 2
            received = tuple(swap(v[split:], "dp", bit) for v in held)
            held = tuple(
                a[:split].astype(F32) + b.astype(F32)
                for a, b in zip(held, received, strict=True)
            )
            bit *= 2
            if bit < dp:
                held = tuple(v.astype(BF16) for v in held)
        gate, up = (v.astype(F32) for v in held)
        return (jax.nn.silu(gate) * up).astype(BF16)

    def gather_units(hidden):
        if tensor != 2:
            return lax.all_gather(hidden, "tensor", axis=1, tiled=True)
        other = swap(hidden, "tensor", 1)
        first = lax.axis_index("tensor") == 0
        return jnp.concatenate(
            (jnp.where(first, hidden, other), jnp.where(first, other, hidden)), axis=1
        )

    def layer_sum(copy, held):
        partial = down_project(gather_units(hidden_of(held)), down_weight, copy, mp)
        return lax.psum_scatter(partial, "mp", scatter_dimension=0, tiled=False)

    def by_features(summed):
        share = summed.shape[1] // dp

        def share_of(owner):
            return lax.dynamic_slice_in_dim(summed, owner * share, share, 1)

        arrived = [share_of(me)] + [
            lax.ppermute(share_of(me ^ j), "dp", [(i, i ^ j) for i in range(dp)])
            for j in range(1, dp)
        ]
        stacked = jnp.stack(arrived)
        bit = 1
        while bit < dp:
            turned = jnp.stack([stacked[j ^ bit] for j in range(dp)])
            stacked = jnp.where((me // bit) % 2 == 1, turned, stacked)
            bit *= 2
        return stacked.reshape(dp * group, share)

    held, last = {}, ()
    for chunk in range(CHUNKS):
        for copy in (1, 0):
            held[copy, chunk] = near_sum(copy, chunk, after(token_groups[chunk], last))
            last = held[copy, chunk]
    summed = {key: layer_sum(key[0], value) for key, value in held.items()}
    inst = [by_features(after(summed[1, 0], last))]
    base = [by_features(after(summed[0, 0], last))]
    share = inst[0].shape[1]
    spot = lax.axis_index(("mp", "dp"))
    sketch_rows = lax.dynamic_slice_in_dim(sketch, spot * share, share, 0)
    rank = sketch.shape[1]

    def inner_of(chunk):
        return jnp.dot(inst[chunk], sketch_rows, preferred_element_type=F32).astype(BF16)

    def outer_of(left, right):
        return lax.dot_general(
            left, right, (((1,), (1,)), ((), ())), preferred_element_type=F32
        ).astype(BF16)

    core = bits_of("dp")[:1]
    far = bits_of("dp")[1:]
    ways = [
        core + far + bits_of("tensor") + bits_of("mp"),
        core + bits_of("tensor") + bits_of("mp") + far,
        core + bits_of("mp") + far + bits_of("tensor"),
    ]
    rows = tokens_all // CHUNKS
    early = jnp.concatenate(
        (inner_of(0), outer_of(inst[0], inst[0]), outer_of(base[0], base[0])), axis=1
    )
    early = gather_halves(reduce_halves(early, ways[0])[0], ways[0])
    inst.append(by_features(after(summed[1, 1], early)))
    inner_0, inst_00, base_00 = early[:, :rank], early[:, rank : rank + rows], early[:, rank + rows :]
    inner_1, inner_steps = reduce_halves(inner_of(1), ways[0])
    inst_1, inst_steps = reduce_halves(outer_of(inst[1], jnp.concatenate(inst)), ways[1])
    base.append(by_features(after(summed[0, 1], (inner_steps[1], inst_steps[1]))))
    base_1, _ = reduce_halves(outer_of(base[1], jnp.concatenate(base)), ways[2])
    inner_1 = gather_halves(inner_1, ways[0])
    inst_1 = gather_halves(inst_1, ways[1])
    base_1 = gather_halves(base_1, ways[2])

    def assemble(first, lower):
        upper = jnp.concatenate((first, lower[:, :rows].T), axis=1)
        return jnp.concatenate((upper, lower), axis=0)

    inner = jnp.concatenate((inner_0, inner_1), axis=0)
    base_outer = assemble(base_00, base_1)
    inst_outer = assemble(inst_00, inst_1)
    inst, base = jnp.concatenate(inst), jnp.concatenate(base)

    scale = 1.0 / (tokens_all * tokens_all * width)

    def round_of(outer_matrix, inner_sums):
        moved = split_dot(outer_matrix, inner_sums)
        gram = lax.dot_general(
            inner_sums, moved, (((0,), (0,)), ((), ())), precision=HIGH
        ) * scale
        return moved, factor_inverse(gram)

    def turn(matrix, inverse):
        return lax.dot_general(matrix, inverse, (((1,), (1,)), ((), ())), precision=HIGH) / tokens_all

    moved, inverse = round_of(base_outer, inner.astype(F32))
    second_inner = turn(moved, inverse)
    moved, inverse = round_of(inst_outer, second_inner)
    third_inner = turn(moved, inverse)
    moved, inverse = round_of(base_outer, third_inner)
    basis_inner = turn(third_inner, inverse).astype(BF16)
    last_inner = (turn(moved, inverse) / tokens_all).astype(BF16)

    def outputs(inner_sums, acts):
        return lax.dot_general(
            inner_sums, acts, (((0,), (0,)), ((), ())), preferred_element_type=F32
        ).astype(BF16)

    both = jnp.stack((outputs(basis_inner, base), outputs(last_inner, inst)))
    shares = mp * dp
    both = both.reshape(2, shares, rank // shares, share).transpose(1, 0, 2, 3)
    both = lax.all_to_all(both, ("mp", "dp"), 0, 0, tiled=True)
    both = both.transpose(1, 0, 3, 2).reshape(2, shares * share, rank // shares).astype(F32)
    return both[0], both[1]


def solution(mesh):
    return jax.shard_map(
        on_device,
        mesh=mesh,
        in_specs=(
            P(("mp", "tensor"), "dp"),
            P(),
            P(None, "dp", ("mp", "tensor")),
            P(None, "dp", ("mp", "tensor")),
            P(None, "mp", "tensor"),
            P("tensor", None),
        ),
        out_specs=(P("tensor", ("mp", "dp")), P("tensor", ("mp", "dp"))),
        check_vma=False,
    )
```
